128 devices in a mesh: row: 8 (over y, core), col: 16 (over z, x).
Axes of the slice: x: 4, y: 4, z: 4, core: 2. Of those that a mesh axis runs over, the one named last changes fastest.
Arguments:
- tokens: bfloat16 [2048, 8192], P('col', 'row'), may hold values from -6 to 6
- query_weight: bfloat16 [8192, 8192], P('row', 'col'), may hold values from -0.0625 to 0.0625
- key_weight: bfloat16 [8192, 8192], P('row', 'col'), may hold values from -0.0625 to 0.0625
- value_weight: bfloat16 [8192, 8192], P('row', 'col'), may hold values from -0.0625 to 0.0625
- out_weight: bfloat16 [8192, 8192], P('col', 'row'), may hold values from -0.0625 to 0.0625
- filter_taps: float32 [7, 512], P(None, 'col'), may hold values from -4 to 4
- out_grad: bfloat16 [2048, 8192], P('col', 'row'), may hold values from -6 to 6
Outputs:
- block_out: bfloat16 [2048, 8192], P('col', 'row')
- tokens_grad: bfloat16 [2048, 8192], P('col', 'row')
- query_grad: bfloat16 [8192, 8192], P('row', 'col')
- key_grad: bfloat16 [8192, 8192], P('row', 'col')
- value_grad: bfloat16 [8192, 8192], P('row', 'col')
- outw_grad: bfloat16 [8192, 8192], P('col', 'row')
- taps_grad: float32 [7, 512], P(None, 'col')
The draws below stay inside these ranges and needn't reach their ends.
All inputs are finite; a program needn't handle non-finite values.
Results may differ from the reference program's by a relative error of at most 0.035.
Values may be sent and summed in bfloat16 or wider, within the bound.
No kernel may reach another device: no remote copies, remote signals or barrier semaphores. Data moves between devices by JAX's collectives and lax.ppermute only.
A program may use at most 128 MiB of HBM per device.

```python
import jax
import jax.numpy as jnp
from jax import lax

D = 8192
KW = 7
GROUP = 16
TOKENS = 2048
LENGTH = 2048
GROUPS = 512
N_ROW = 8


def shard_levels(key, extent, split, least, top_value):
    loudness, own = 1.0, jax.random.fold_in(key, 6)
    for axis_at, shards_of in split:
        draws = jnp.exp(jax.random.uniform(jax.random.fold_in(own, axis_at), (shards_of,), jnp.float32, least / len(split), top_value / len(split)))
        loudness = loudness * jnp.repeat(draws, extent[axis_at] // shards_of).reshape([-1 if axis == axis_at else 1 for axis in range(len(extent))])
    return loudness


def centred(own_key, shape, scale, most, split=(), kind=jnp.bfloat16):
    result = scale * jax.random.normal(own_key, shape, jnp.float32)
    if split:
        result = result * shard_levels(own_key, shape, split, -0.22, 0.18)
    return jnp.clip(result, -most, most).astype(kind)


def setup_inputs(seed: int = 0) -> dict:
    splits = jax.random.split(jax.random.key(seed), 8)
    return {
        "tokens": centred(splits[0], (TOKENS, D), 1.0, 6.0, ((0, 16), (1, 8))),
        "query_weight": centred(splits[1], (D, D), D ** -0.5, 0.0625, ((0, 8), (1, 16))),
        "key_weight": centred(splits[2], (D, D), D ** -0.5, 0.0625, ((0, 8), (1, 16))),
        "value_weight": centred(splits[3], (D, D), D ** -0.5, 0.0625, ((0, 8), (1, 16))),
        "out_weight": centred(splits[4], (D, D), D ** -0.5, 0.0625, ((0, 16), (1, 8))),
        "filter_taps": centred(splits[5], (KW, GROUPS), 0.4, 4.0, ((1, 16),), jnp.float32),
        "out_grad": centred(splits[6], (TOKENS, D), 1.0, 6.0, ((0, 16), (1, 8))),
    }


def causal_conv(signal, taps, positions):
    count_rows = signal.shape[0]
    padded = jnp.pad(signal, ((KW - 1, 0), (0, 0)))
    total = jnp.zeros(signal.shape, jnp.float32)
    for offset in range(KW):
        shifted = padded[KW - 1 - offset:KW - 1 - offset + count_rows]
        keep = (positions % LENGTH >= offset)[:, None]
        total = total + jnp.where(keep, taps[offset][None, :] * shifted, 0.0)
    return total


def causal_conv_back(cotangent, taps, positions):
    count_rows = cotangent.shape[0]
    padded = jnp.pad(cotangent, ((0, KW - 1), (0, 0)))
    total = jnp.zeros(cotangent.shape, jnp.float32)
    for offset in range(KW):
        shifted = padded[offset:offset + count_rows]
        keep = ((positions % LENGTH) + offset < LENGTH)[:, None]
        total = total + jnp.where(keep, taps[offset][None, :] * shifted, 0.0)
    return total


def blockwise(left, right_fn, width_out):
    block = D // N_ROW
    total = jnp.zeros((left.shape[0], width_out), jnp.float32)
    for shard in range(N_ROW):
        partial_value = right_fn(left[:, shard * block:(shard + 1) * block], shard * block, block).astype(jnp.bfloat16)
        total = total + lax.optimization_barrier(partial_value).astype(jnp.float32)
    return total.astype(jnp.bfloat16)


def reference(tokens, query_weight, key_weight, value_weight, out_weight, filter_taps, out_grad):
    def projector(weight):
        def apply(columns, first, width):
            return jnp.dot(columns, weight[first:first + width], preferred_element_type=jnp.float32)
        return apply

    query = blockwise(tokens, projector(query_weight), D)
    keys = blockwise(tokens, projector(key_weight), D)
    values = blockwise(tokens, projector(value_weight), D)
    product = (keys.astype(jnp.float32) * values.astype(jnp.float32)).astype(jnp.bfloat16)
    taps = jnp.repeat(filter_taps.astype(jnp.float32), GROUP, axis=1)
    positions = jnp.arange(TOKENS, dtype=jnp.int32)
    conv_out = causal_conv(product.astype(jnp.float32), taps, positions).astype(jnp.bfloat16)
    gated = (query.astype(jnp.float32) * conv_out.astype(jnp.float32)).astype(jnp.bfloat16)
    block_out = jnp.dot(gated, out_weight, preferred_element_type=jnp.float32).astype(jnp.bfloat16)

    def back_apply(columns, first, width):
        return jnp.dot(columns, out_weight[:, first:first + width].T, preferred_element_type=jnp.float32)

    gated_grad = blockwise(out_grad, back_apply, D)
    query_back = (gated_grad.astype(jnp.float32) * conv_out.astype(jnp.float32)).astype(jnp.bfloat16)
    conv_grad = (gated_grad.astype(jnp.float32) * query.astype(jnp.float32)).astype(jnp.bfloat16)
    product_grad = causal_conv_back(conv_grad.astype(jnp.float32), taps, positions)
    keys_back = (product_grad * values.astype(jnp.float32)).astype(jnp.bfloat16)
    values_back = (product_grad * keys.astype(jnp.float32)).astype(jnp.bfloat16)

    padded = jnp.pad(product.astype(jnp.float32), ((KW - 1, 0), (0, 0)))
    rows_grad = []
    for offset in range(KW):
        shifted = padded[KW - 1 - offset:KW - 1 - offset + TOKENS]
        keep = (positions % LENGTH >= offset)[:, None]
        rows_grad.append(jnp.sum(jnp.where(keep, conv_grad.astype(jnp.float32) * shifted, 0.0), axis=0))
    taps_grad = jnp.stack(rows_grad).reshape(KW, GROUPS, GROUP).sum(axis=2)

    query_grad = jnp.dot(tokens.T, query_back, preferred_element_type=jnp.float32).astype(jnp.bfloat16)
    key_grad = jnp.dot(tokens.T, keys_back, preferred_element_type=jnp.float32).astype(jnp.bfloat16)
    value_grad = jnp.dot(tokens.T, values_back, preferred_element_type=jnp.float32).astype(jnp.bfloat16)
    outw_grad = jnp.dot(gated.T, out_grad, preferred_element_type=jnp.float32).astype(jnp.bfloat16)
    tokens_grad = (jnp.dot(query_back, query_weight.T, preferred_element_type=jnp.float32)
                   + jnp.dot(keys_back, key_weight.T, preferred_element_type=jnp.float32)
                   + jnp.dot(values_back, value_weight.T, preferred_element_type=jnp.float32)).astype(jnp.bfloat16)
    return block_out, tokens_grad, query_grad, key_grad, value_grad, outw_grad, taps_grad
```

```python
import jax
import jax.numpy as jnp
from jax import lax
from jax.experimental import pallas as pl
from jax.experimental.pallas import tpu as pltpu
from jax.sharding import Mesh, PartitionSpec as P

KW = 7
GROUP = 16
AXES = ("y", "core", "z", "x")
NY, NC, NZ, NX = 4, 2, 4, 4
BF = jnp.bfloat16
F32 = jnp.float32


def permute(value, move):
    def flat(y, c, z, x):
        return ((y % NY * NC + c) * NZ + z % NZ) * NX + x % NX

    pairs = [
        (flat(y, c, z, x), flat(*move(y, c, z, x)))
        for y in range(NY)
        for c in range(NC)
        for z in range(NZ)
        for x in range(NX)
    ]
    return lax.ppermute(value, AXES, pairs)


def swap_cores(value):
    return permute(value, lambda y, c, z, x: (y, 1 - c, z, x))


def along_first(value, by):
    return permute(value, lambda y, c, z, x: (y, c, z, x + by) if c == 0 else (y, c, z + by, x))


def along_second(value, by):
    return permute(value, lambda y, c, z, x: (y, c, z + by, x) if c == 0 else (y, c, z, x + by))


def round_row(value):
    return permute(value, lambda y, c, z, x: (y + 1, c, z, x) if c == 0 else (y - 1, c, z, x))


def place(pieces, at):
    total = jnp.zeros((4,) + pieces[0].shape, pieces[0].dtype)
    for k, piece in enumerate(pieces):
        total = lax.dynamic_update_slice(
            total, piece[None], ((at + k) % 4,) + (0,) * piece.ndim
        )
    return total


def gather_axis(value, shift, at):
    ahead = shift(value, -1)
    behind = shift(value, 1)
    across = shift(value, 2)
    return place([value, ahead, across, behind], at)


def gather_col(shard, core, first, second):
    wide = gather_axis(shard, along_first, first)
    full = gather_axis(wide, along_second, second)
    full = jnp.where(core == 0, full, jnp.swapaxes(full, 0, 1))
    return full.reshape((-1, shard.shape[1]))


def pick(value, index):
    return lax.dynamic_index_in_dim(value, index % 4, 0, keepdims=False)


def scatter_axis(parts, shift, at):
    across = shift(pick(parts, at + 2), 2)
    ahead = shift(pick(parts, at + 1), 1)
    behind = shift(pick(parts, at + 3), -1)
    own = pick(parts, at).astype(F32)
    return (own + across.astype(F32) + ahead.astype(F32) + behind.astype(F32)).astype(BF)


def scatter_col(full, core, first, second):
    parts = full.reshape((4, 4, -1, full.shape[1]))
    parts = jnp.where(core == 0, parts, jnp.swapaxes(parts, 0, 1))
    kept = scatter_axis(parts, along_second, second)
    return scatter_axis(kept, along_first, first)


def contract(left, right, dims):
    return lax.dot_general(left, right, ((dims[:1], dims[1:]), ((), ())), preferred_element_type=F32)


def scatter_row(weight_blocks, rows, core, y):
    n = weight_blocks.shape[1]
    step_own = jnp.where(core == 0, 3, 1)
    carried = None
    for step in range(4):
        own_at = 2 * ((y + step_own * (step + 1)) % 4) + core
        other_at = 2 * ((y + (4 - step_own) * (step + 1)) % 4) + 1 - core
        own_w = lax.dynamic_index_in_dim(weight_blocks, own_at, 0, keepdims=False)
        other_w = lax.dynamic_index_in_dim(weight_blocks, other_at, 0, keepdims=False)
        both = contract(jnp.concatenate([own_w, other_w], axis=0), rows, (1, 1))
        received = swap_cores(both[n:].astype(BF))
        total = both[:n].astype(BF).astype(F32) + received.astype(F32)
        if carried is not None:
            total = total + carried.astype(F32)
        total = total.astype(BF)
        if step < 3:
            carried = round_row(total)
    return total


def gather_row(shard, core, y):
    step_own = jnp.where(core == 0, 3, 1)
    total = jnp.zeros((8,) + shard.shape, shard.dtype)
    chunk = shard
    for step in range(4):
        if step == 0:
            own_at, other_at = 2 * y + core, 2 * y + 1 - core
        else:
            chunk = round_row(chunk)
            own_at = 2 * ((y + step_own * step) % 4) + core
            other_at = 2 * ((y + (4 - step_own) * step) % 4) + 1 - core
        other = swap_cores(chunk)
        total = lax.dynamic_update_slice(total, chunk[None], (own_at, 0, 0))
        total = lax.dynamic_update_slice(total, other[None], (other_at, 0, 0))
    return total


def shifted_down(value, by, lanes):
    if by == 0:
        return value
    return jnp.where(lanes >= by, pltpu.roll(value, by, 1), 0.0)


def shifted_up(value, by, lanes):
    if by == 0:
        return value
    count = value.shape[1]
    return jnp.where(lanes < count - by, pltpu.roll(value, count - by, 1), 0.0)


def forward_kernel(taps_ref, qkv_ref, gated_ref, conv_ref):
    block = pl.program_id(0)
    keys = qkv_ref[1].astype(F32)
    values = qkv_ref[2].astype(F32)
    product = (keys * values).astype(BF).astype(F32)
    lanes = lax.broadcasted_iota(jnp.int32, product.shape, 1)
    total = taps_ref[0, block] * product
    for by in range(1, KW):
        total = total + taps_ref[by, block] * shifted_down(product, by, lanes)
    conv_out = total.astype(BF)
    conv_ref[...] = conv_out
    gated_ref[...] = (qkv_ref[0].astype(F32) * conv_out.astype(F32)).astype(BF)


def backward_kernel(taps_ref, qkv_ref, conv_ref, grad_ref, back_ref, taps_grad_ref):
    block = pl.program_id(0)
    query = qkv_ref[0].astype(F32)
    keys = qkv_ref[1].astype(F32)
    values = qkv_ref[2].astype(F32)
    grad = grad_ref[...].astype(F32)
    product = (keys * values).astype(BF).astype(F32)
    lanes = lax.broadcasted_iota(jnp.int32, product.shape, 1)
    back_ref[0] = (grad * conv_ref[...].astype(F32)).astype(BF)
    conv_grad = (grad * query).astype(BF).astype(F32)
    total = taps_ref[0, block] * conv_grad
    rows = [jnp.sum(conv_grad * product, axis=(0, 1), keepdims=True)]
    for by in range(1, KW):
        total = total + taps_ref[by, block] * shifted_up(conv_grad, by, lanes)
        rows.append(
            jnp.sum(conv_grad * shifted_down(product, by, lanes), axis=(0, 1), keepdims=True)
        )
    back_ref[1] = (total * values).astype(BF)
    back_ref[2] = (total * keys).astype(BF)
    rows.append(jnp.zeros((1, 1), F32))
    taps_grad_ref[0] = jnp.broadcast_to(jnp.concatenate(rows, axis=0), (8, 128))


def forward_stage(taps, qkv):
    _, channels, tokens = qkv.shape
    return pl.pallas_call(
        forward_kernel,
        grid=(channels // GROUP,),
        in_specs=[
            pl.BlockSpec(memory_space=pltpu.SMEM),
            pl.BlockSpec((3, GROUP, tokens), lambda i: (0, i, 0)),
        ],
        out_specs=[
            pl.BlockSpec((GROUP, tokens), lambda i: (i, 0)),
            pl.BlockSpec((GROUP, tokens), lambda i: (i, 0)),
        ],
        out_shape=[jax.ShapeDtypeStruct((channels, tokens), BF)] * 2,
        name="hyena_forward",
    )(taps, qkv)


def backward_stage(taps, qkv, conv_out, grad):
    _, channels, tokens = qkv.shape
    groups = channels // GROUP
    return pl.pallas_call(
        backward_kernel,
        grid=(groups,),
        in_specs=[
            pl.BlockSpec(memory_space=pltpu.SMEM),
            pl.BlockSpec((3, GROUP, tokens), lambda i: (0, i, 0)),
            pl.BlockSpec((GROUP, tokens), lambda i: (i, 0)),
            pl.BlockSpec((GROUP, tokens), lambda i: (i, 0)),
        ],
        out_specs=[
            pl.BlockSpec((3, GROUP, tokens), lambda i: (0, i, 0)),
            pl.BlockSpec((1, 8, 128), lambda i: (i, 0, 0)),
        ],
        out_shape=[
            jax.ShapeDtypeStruct((3, channels, tokens), BF),
            jax.ShapeDtypeStruct((groups, 8, 128), F32),
        ],
        name="hyena_backward",
    )(taps, qkv, conv_out, grad)


def local(tokens, query_weight, key_weight, value_weight, out_weight, filter_taps, out_grad):
    y, core, z, x = (lax.axis_index(name) for name in AXES)
    first = jnp.where(core == 0, x, z)
    second = jnp.where(core == 0, z, x)
    features, hidden = query_weight.shape
    rows_each = hidden // 8
    row = 2 * y + core

    full_tokens = gather_col(tokens, core, first, second)
    count = full_tokens.shape[0]
    joined = jnp.stack(
        [w.T.reshape(8, rows_each, features) for w in (query_weight, key_weight, value_weight)],
        axis=1,
    )
    qkv = scatter_row(joined.reshape(8, 3 * rows_each, features), full_tokens, core, y)
    qkv = qkv.reshape(3, rows_each, count)
    groups = filter_taps.shape[1] // 8
    taps = lax.dynamic_slice(filter_taps, (0, row * groups), (KW, groups))
    gated, conv_out = forward_stage(taps, qkv)

    full_grad = gather_col(out_grad, core, first, second)
    gated_grad = scatter_row(out_weight.reshape(8, rows_each, -1), full_grad, core, y)

    gated_all = gather_row(gated, core, y).reshape(hidden, count)
    block_full = contract(gated_all, out_weight, (0, 0)).astype(BF)
    block_out = scatter_col(block_full, core, first, second)

    back, taps_blocks = backward_stage(taps, qkv, conv_out, gated_grad)
    back_all = gather_row(back.reshape(3 * rows_each, count), core, y).reshape(3 * hidden, count)
    tokens_full = contract(back_all, joined.reshape(3 * hidden, features), (0, 0)).astype(BF)
    tokens_grad = scatter_col(tokens_full, core, first, second)

    weight_grads = contract(back_all, full_tokens, (1, 0)).astype(BF)
    weight_grads = weight_grads.reshape(8, 3, rows_each, features)
    query_grad, key_grad, value_grad = (
        weight_grads[:, i].reshape(hidden, features).T for i in range(3)
    )
    outw_grad = contract(gated_all, full_grad, (1, 0)).astype(BF)

    taps_mine = taps_blocks[:, :KW, 0]
    taps_all = gather_row(jnp.pad(taps_mine, ((0, 0), (0, 128 - KW))), core, y)
    taps_grad = taps_all.reshape(8 * groups, 128)[:, :KW].T
    return (block_out, tokens_grad, query_grad, key_grad, value_grad, outw_grad, taps_grad)


def solution(mesh):
    fine = Mesh(mesh.devices.reshape(NY, NC, NZ, NX), AXES)
    row, col = ("y", "core"), ("z", "x")
    in_specs = (
        P(col, row),
        P(row, col),
        P(row, col),
        P(row, col),
        P(col, row),
        P(None, col),
        P(col, row),
    )
    out_specs = (
        P(col, row),
        P(col, row),
        P(row, col),
        P(row, col),
        P(row, col),
        P(col, row),
        P(None, col),
    )
    return jax.shard_map(local, mesh=fine, in_specs=in_specs, out_specs=out_specs, check_vma=False)
```
